32 devices in a mesh: row: 4 (over z), col: 8 (over y, x, core).
Axes of the slice: x: 2, y: 2, z: 4, core: 2. Of those that a mesh axis runs over, the one named last changes fastest.
Arguments:
- rhs_front: float32 [4, 6144, 1024], P(None, 'row', 'col'), may hold values from -6 to 6
- lower_blocks: float32 [6, 6144, 6144], P(None, 'row', 'col'), may hold values from -0.046875 to 0.046875
- panel_inverse: float32 [4, 6144, 6144], P(None, 'col', 'row'), may hold values from -0.078125 to 0.078125
- child_rows: float32 [4, 64, 128, 1024], P('row', 'col'), may hold values from -4 to 4
- child_map: int32 [4, 64], P('row', 'col'), may hold values from 0 to 47
- child_owner: int32 [8, 24, 1], P('col'), may hold values from 0 to 3; in each aligned block of 24 rows (0 to 23, 24 to 47, ..., all dimensions but the last counted through in order) at most 7 rows name the same one
Outputs:
- solution: float32 [4, 6144, 1024], P(None, 'col')
- child_rhs: float32 [8, 4, 7, 128, 1024], P('col', 'row')
The draws below stay inside these ranges and needn't reach their ends.
Inputs may be any that keep to these rules, and one draw needn't show every extreme that they name: `child_map`: several child update blocks may name the same front block. `child_owner`: of the 24 solved blocks of one column group, at most 7 name the same row group, and in some column group one row group is named exactly 7 times.
All inputs are finite; a program needn't handle non-finite values.
Results may differ from the reference program's by a relative error of at most 0.00012.
Values sent between devices are 32-bit elements; how exact they have to be, the bound alone decides.
A program may use at most 192 MiB of HBM per device.

```python
import math
import jax
import jax.numpy as jnp
import numpy as np
from jax import lax

PANELS = 4
BLOCK = 128
R = 1024
CB_DEV = 8
PW = 6144
NLOW = 6
LB = 48
BPC = 6
BLK_DEV = 24
MOST = 7
N_ROW = 4
N_COL = 8


def with_ends(array, own_key, low, high):
    index_at = [jax.random.randint(jax.random.fold_in(own_key, axis), (), 0, length) for axis, length in enumerate(array.shape)]
    main_axis = array.shape.index(max(array.shape))
    next_to = index_at[:main_axis] + [(index_at[main_axis] + 1) % array.shape[main_axis]] + index_at[main_axis + 1:]
    return array.at[tuple(index_at)].set(low).at[tuple(next_to)].set(high)


def block_levels(key, dims, split, low, largest):
    loudness, own = 1.0, jax.random.fold_in(key, 6)
    for position, blocks in split:
        draws = jnp.exp(jax.random.uniform(jax.random.fold_in(own, position), (blocks,), jnp.float32, low / len(split), largest / len(split)))
        loudness = loudness * jnp.repeat(draws, dims[position] // blocks).reshape([-1 if axis == position else 1 for axis in range(len(dims))])
    return loudness


def shared_out(key, own, number, rows, amount, top, most, slope):
    order = jax.random.permutation(key, amount)
    crowded, ordinary = load_shares(amount, rows * top, most, slope, True), load_shares(amount, rows * top, most, slope, False)
    places = jnp.arange(amount)

    def named(lengths, rotation):
        used = int((lengths > 0).sum())
        fixed = max(1, used // 4)
        passed = fixed + (places - fixed + rotation * (used - fixed)) % max(1, amount - fixed)
        return jnp.zeros((amount,), jnp.int32).at[order[jnp.where(places < fixed, places, passed)]].set(jnp.asarray(lengths, jnp.int32))

    lengths = jnp.where(number % 4 == 0, named(crowded, number // 4), named(ordinary, number - number // 4 - 1))
    mixed = jax.random.permutation(jax.random.fold_in(own, 3), amount)
    donor, sink = mixed[0:amount // 2 * 2:2], mixed[1:amount // 2 * 2:2]
    room = jnp.minimum(lengths[donor] - 1, most - lengths[sink]) // 2
    room = jnp.where((donor == order[0]) | (sink == order[0]) | (lengths[sink] == 0), 0, jnp.maximum(room, 0))
    passed = jax.random.randint(jax.random.fold_in(own, 4), (amount // 2,), 0, 1 << 20) % (room + 1)
    lengths = lengths.at[donor].add(-passed).at[sink].add(passed)
    labels = jnp.searchsorted(jnp.cumsum(lengths), jnp.arange(rows * top), side="right").astype(jnp.int32)
    listing = labels.reshape(top, rows).T
    listing = listing[jax.random.permutation(jax.random.fold_in(own, 1), rows)]
    rotation = jax.random.randint(jax.random.fold_in(own, 2), (rows, 1), 0, top)
    return jnp.take_along_axis(listing, (jnp.arange(top)[None, :] + rotation) % top, axis=1)


def load_shares(number_of, total, limit, skew, full):
    loads = [(1 << 20) // math.isqrt(standing ** skew) + 1 for standing in range(1, number_of + 1)]
    largest = limit if full else min(limit, max(-(-total // number_of), total * loads[0] // sum(loads)))
    least = 1 if total - largest >= number_of - 1 else 0
    counts, surplus = [largest] + [least] * (number_of - 1), total - largest - least * (number_of - 1)
    while surplus > 0:
        movable = [i for i in range(1, number_of) if counts[i] < largest] or [i for i in range(1, number_of) if counts[i] < limit]
        mass, left = sum([loads[i] for i in movable]), surplus
        for i in movable:
            addition = min(limit - counts[i], max(1, left * loads[i] // mass), surplus)
            counts[i] = counts[i] + addition
            surplus = surplus - addition
    return np.array(counts)


def scatter_about(key, dims, width, limit, shards=(), kind=jnp.bfloat16):
    gain = block_levels(key, dims, shards, -0.22, 0.18) if shards else 1.0
    entries = jax.random.normal(key, dims, jnp.float32) * width * gain
    return jnp.minimum(jnp.maximum(entries, -limit), limit).astype(kind)


def setup_inputs(seed: int = 0) -> dict:
    seeds = jax.random.split(jax.random.key(seed), 7)
    rhs_front = scatter_about(seeds[0], (PANELS, PW, R), 1.0, 6.0, ((1, 4), (2, 8)), jnp.float32)
    lower_blocks = scatter_about(seeds[1], (NLOW, PW, PW), (3 * PW) ** -0.5, 0.046875, ((1, 4), (2, 8)), jnp.float32)
    panel_inverse = scatter_about(seeds[2], (PANELS, PW, PW), PW ** -0.5, 0.078125, ((1, 8), (2, 4)), jnp.float32)
    child_rows = scatter_about(seeds[3], (N_ROW, N_COL * CB_DEV, BLOCK, R), 0.5, 4.0, ((0, 4), (1, 8)), jnp.float32)
    child_map = with_ends(jax.random.randint(seeds[4], (N_ROW, N_COL * CB_DEV), 0, LB), jax.random.fold_in(seeds[4], 1), 0, LB - 1).astype(jnp.int32)
    child_owner_keys = jax.random.split(jax.random.fold_in(seeds[5], 1), N_COL * BLK_DEV // BLK_DEV)
    child_owner_turns = jax.random.permutation(jax.random.fold_in(seeds[5], 3), N_COL * BLK_DEV // BLK_DEV)
    child_owner = jax.vmap(lambda own, number: shared_out(jax.random.fold_in(seeds[5], 2), own, number, BLK_DEV, N_ROW, 1, MOST, 1))(child_owner_keys, child_owner_turns).reshape((N_COL, BLK_DEV, 1))
    return {"rhs_front": rhs_front, "lower_blocks": lower_blocks, "panel_inverse": panel_inverse, "child_rows": child_rows, "child_map": child_map, "child_owner": child_owner}


def reference(rhs_front, lower_blocks, panel_inverse, child_rows, child_map, child_owner):
    highest = lax.Precision.HIGHEST
    row_span = PW // N_ROW
    targets = jnp.arange(LB, dtype=jnp.int32)
    picks = (child_map[:, None, :] == targets[None, :, None]).astype(jnp.float32)
    added = jnp.einsum('rlk,rkbc->rlbc', picks, child_rows, precision=highest)
    added = added.reshape(N_ROW, PANELS, row_span, R).transpose(1, 0, 2, 3).reshape(PANELS, PW, R)
    assembled = rhs_front + added
    solved = []
    for panel in range(PANELS):
        front = assembled[panel]
        for prior in range(panel):
            front = front - jnp.dot(lower_blocks[panel * (panel - 1) // 2 + prior], solved[prior], precision=highest, preferred_element_type=jnp.float32)
        solved.append(jnp.dot(panel_inverse[panel], front, precision=highest, preferred_element_type=jnp.float32))
    solution = jnp.stack(solved)
    blocks = solution.reshape(PANELS, N_COL, BPC, BLOCK, R).transpose(1, 0, 2, 3, 4).reshape(N_COL, BLK_DEV, BLOCK, R)
    owner = child_owner[:, :, 0]
    hits = (owner[:, None, :] == jnp.arange(N_ROW, dtype=jnp.int32)[None, :, None]).astype(jnp.int32)
    ranks = jnp.cumsum(hits, axis=2) - hits
    slot_match = (ranks[:, :, None, :] == jnp.arange(MOST, dtype=jnp.int32)[None, None, :, None]).astype(jnp.int32)
    routing = (hits[:, :, None, :] * slot_match).astype(jnp.float32)
    delivered = jnp.einsum('cdsk,ckbr->cdsbr', routing, blocks, precision=highest)
    return solution, delivered
```

```python
import jax
import jax.numpy as jnp
from jax import lax
from jax.sharding import PartitionSpec as P

CHUNKS = 2


def bits_of(axis):
    return list(range(lax.axis_size(axis).bit_length() - 1))


def swap(value, axis, bit):
    size = lax.axis_size(axis)
    return lax.ppermute(value, axis, [(i, i ^ (1 << bit)) for i in range(size)])


def halve(value, axis, bit):
    mine = (lax.axis_index(axis) >> bit) & 1
    half = value.shape[0] // 2
    sent = lax.dynamic_slice_in_dim(value, (1 - mine) * half, half, 0)
    kept = lax.dynamic_slice_in_dim(value, mine * half, half, 0)
    return kept + swap(sent, axis, bit)


def double(value, axis, bit):
    mine = (lax.axis_index(axis) >> bit) & 1
    other = swap(value, axis, bit)
    low = jnp.where(mine == 0, value, other)
    high = jnp.where(mine == 0, other, value)
    return jnp.concatenate([low, high], axis=0)


def sum_in_order(value, axis, bits):
    for bit in bits:
        value = halve(value, axis, bit)
    for bit in reversed(bits):
        value = double(value, axis, bit)
    return value


def sum_over_row(value):
    return sum_in_order(value, "row", bits_of("row"))


def sum_over_col(value):
    bits = bits_of("col")
    part = halve(value, "col", bits[0])
    half = part.shape[0] // 2
    rest = bits[1:]
    first = sum_in_order(part[:half], "col", rest)
    second = sum_in_order(part[half:], "col", rest[::-1])
    return double(jnp.concatenate([first, second], axis=0), "col", bits[0])


def on_device(rhs_front, lower_blocks, panel_inverse, child_rows, child_map, child_owner):
    high = lax.Precision.HIGH
    row_count = lax.axis_size("row")
    row_at = lax.axis_index("row")
    col_at = lax.axis_index("col")
    panels, row_span, narrow = rhs_front.shape
    col_span = panel_inverse.shape[1]
    held_children, block, width = child_rows.shape[1:]
    local_blocks = panels * row_span // block
    per_panel = col_span // block
    held_blocks = panels * per_panel
    most = max(2, held_blocks // row_count + 1)
    assembled = lax.dynamic_update_slice(
        jnp.zeros((panels, row_span, width), jnp.float32), rhs_front, (0, 0, col_at * narrow)
    ).reshape(local_blocks, block, width)
    for k in range(held_children):
        at = child_map[0, k]
        old = lax.dynamic_slice_in_dim(assembled, at, 1, 0)
        assembled = lax.dynamic_update_slice_in_dim(assembled, old + child_rows[0, k][None], at, 0)
    assembled = assembled.reshape(panels, row_span, width)
    piece = width // CHUNKS
    solved = [[] for _ in range(CHUNKS)]
    for panel in range(panels):
        for c in range(CHUNKS):
            front = lax.slice_in_dim(assembled[panel], c * piece, (c + 1) * piece, axis=1)
            for prior in range(panel):
                front = front - jnp.dot(
                    lower_blocks[panel * (panel - 1) // 2 + prior],
                    solved[c][prior],
                    precision=high,
                    preferred_element_type=jnp.float32,
                )
            front = sum_over_col(front)
            partial_value = jnp.dot(
                panel_inverse[panel], front, precision=high, preferred_element_type=jnp.float32
            )
            solved[c].append(sum_over_row(partial_value))
    solution = jnp.concatenate([jnp.stack(s) for s in solved], axis=2)
    blocks = solution.reshape(held_blocks, block, width)
    mine = (child_owner[0, :, 0] == row_at).astype(jnp.int32)
    ranks = jnp.cumsum(mine) - mine
    slots = jnp.arange(most, dtype=jnp.int32)
    match = mine[None, :] * (ranks[None, :] == slots[:, None]).astype(jnp.int32)
    source = jnp.sum(match * jnp.arange(held_blocks, dtype=jnp.int32)[None, :], axis=1)
    filled = jnp.sum(match, axis=1) > 0
    received = jnp.stack(
        [
            jnp.where(filled[s], lax.dynamic_index_in_dim(blocks, source[s], 0, False), 0.0)
            for s in range(most)
        ]
    )
    return (solution, received.reshape(1, 1, most, block, width))


def solution(mesh):
    return jax.shard_map(
        on_device,
        mesh=mesh,
        in_specs=(
            P(None, "row", "col"),
            P(None, "row", "col"),
            P(None, "col", "row"),
            P("row", "col", None, None),
            P("row", "col"),
            P("col", None, None),
        ),
        out_specs=(P(None, "col", None), P("col", "row", None, None, None)),
        check_vma=False,
    )
```
